1024 devices in a mesh: band: 16 (over y_hi, x), grid: 64 (over z, y_lo, core).
Axes of the slice: x: 8, y: 8 (y_hi: 2, y_lo: 4; y = y_hi * 4 + y_lo), z: 8, core: 2. Of those that a mesh axis runs over, the one named last changes fastest.
Arguments:
- resident: float32 [16, 128, 128, 128], P('band', 'grid'), may hold values from -2 to 2
- occupied: float32 [32, 128, 128, 128], P('band', 'grid'), may hold values from -2 to 2
Outputs:
- exchange_field: float32 [16, 128, 128, 128], P('band', 'grid')
The draws below stay inside these ranges and needn't reach their ends.
All inputs are finite; a program needn't handle non-finite values.
Results may differ from the reference program's by a relative error of at most 0.0003.
Values sent between devices are 32-bit elements; how exact they have to be, the bound alone decides.
A program may use at most 32 MiB of HBM per device.

```python
import math
import jax
import jax.numpy as jnp
from jax import lax

NX = 128
NY = 128
NZ = 128
RES = 1
VIS = 2
TURNS = 3
BANDS = 16
OCC = 32


def draw_field(base_key, rows_count, salt_value):
    folded = jax.random.fold_in(base_key, salt_value)
    first_key = jax.random.fold_in(folded, 0)
    full_shape = (rows_count, NX, NY, NZ)
    values_out = 0.5 * jax.random.normal(first_key, full_shape, jnp.float32)
    return jnp.clip(values_out, -2.0, 2.0)


def draw_resident(key, part):
    return draw_field(key, BANDS, 11)


def draw_occupied(key, part):
    return draw_field(key, OCC, 23)


def setup_inputs(seed: int = 0) -> dict:
    splits = jax.random.split(jax.random.key(seed), 3)
    resident = draw_resident(jax.random.fold_in(splits[2], 71), 0)
    occupied = draw_occupied(jax.random.fold_in(splits[2], 71), 0)
    return dict(resident=resident, occupied=occupied)


screening = 0.05
mix_fraction = 0.25


def signed_freq(length, modes):
    index = jnp.arange(modes, dtype=jnp.int32)
    return jnp.minimum(index, length - index).astype(jnp.float32) * (2.0 * math.pi / length)


def coulomb_table(modes_z):
    freq_x = signed_freq(NX, NX)
    freq_y = signed_freq(NY, NY)
    freq_z = signed_freq(NZ, modes_z)
    q_square = (freq_x[:, None, None] ** 2 + freq_y[None, :, None] ** 2 + freq_z[None, None, :] ** 2) / (4.0 * screening ** 2)
    positive = q_square > 0
    safe_square = jnp.where(positive, q_square, jnp.ones_like(q_square))
    ratio = jnp.where(positive, -jnp.expm1(-safe_square) / safe_square, jnp.ones_like(q_square))
    return (math.pi / screening ** 2) * ratio


def reference(resident, occupied):
    group_count = OCC // VIS
    groups = occupied.reshape(group_count, VIS, NX, NY, NZ)
    kernel = coulomb_table(NZ // 2 + 1)
    turn_steps = jnp.arange(TURNS, dtype=jnp.int32)

    def one_orbital(orbit_index):
        orbital = resident[orbit_index]
        group_index = orbit_index // RES
        sources = (group_index - turn_steps) % group_count
        visitors = groups[sources].reshape(TURNS * VIS, NX, NY, NZ)
        pair_field = visitors * orbital[None]
        spectrum = jnp.fft.rfftn(pair_field, axes=(1, 2, 3))
        potential = jnp.fft.irfftn(spectrum * kernel[None], s=(NX, NY, NZ), axes=(1, 2, 3))
        return -mix_fraction * jnp.sum(visitors * potential, axis=0)

    return lax.map(one_orbital, jnp.arange(BANDS, dtype=jnp.int32))
```

```python
import functools
import math

import jax
import jax.numpy as jnp
import numpy as np
from jax import lax
from jax.experimental import pallas as pl
from jax.experimental.pallas import tpu as pltpu
from jax.sharding import PartitionSpec as P

N = 128
CELLS = N * N * N
TURNS = 3
BANDS = 16
GRID = 64
screening = 0.05
mix_fraction = 0.25
MESH = pl.DeviceIdType.MESH
F32 = jnp.float32
BF16 = jnp.bfloat16


def split_table(table):
    high = table.astype(np.float32).astype(jnp.bfloat16)
    low = (table - high.astype(np.float64)).astype(np.float32).astype(jnp.bfloat16)
    return [high, low]


def tables():
    index = np.arange(N)
    angle = (index[:, None] * index[None, :] % N) * (2.0 * math.pi / N)
    cas = np.cos(angle) + np.sin(angle)
    along_z = np.kron(np.eye(2), cas)
    along_y = np.zeros((N // 4, 2, 4, 2, N))
    for plane in range(2):
        along_y[:, plane, :, plane, :] = cas.reshape(N // 4, 4, N)
    along_y = along_y.reshape(2 * N, 2 * N)
    out = []
    for table in (along_z, along_y, along_y.T, cas):
        out += split_table(table)
    return out


def halves(value):
    high = value.astype(BF16)
    low = (value - high.astype(F32)).astype(BF16)
    return high, low


def dot(a, b):
    return jnp.dot(a, b, preferred_element_type=F32)


def data_by_table(value, high, low):
    a, b = halves(value)
    return dot(a, high[...]) + (dot(b, high[...]) + dot(a, low[...]))


def table_by_data(high, low, value):
    a, b = halves(value)
    return dot(high[...], a) + (dot(high[...], b) + dot(low[...], a))


def signed_square(index):
    signed = jnp.minimum(index, N - index).astype(F32) * (2.0 * math.pi / N)
    return signed * signed


def kernel(
    res, occ, z_high, z_low, y_high, y_low, yt_high, yt_low, x_high, x_low, out,
    visit, sbuf, rbuf, sback, rback, coef,
    visit_send, visit_recv, send_sem, recv_sem, bsend_sem, brecv_sem,
):
    band = lax.axis_index("band")
    me = lax.axis_index("grid")
    mine = pl.ds(pl.multiple_of(me * 8, 8), 8)

    barrier = pltpu.get_barrier_semaphore()

    def greet(step, carry):
        pl.semaphore_signal(
            barrier, inc=1, device_id={"grid": lax.rem(me + step, GRID)}, device_id_type=MESH
        )
        return carry

    lax.fori_loop(1, GRID, greet, 0)
    for shift in (1, 2, BANDS - 2, BANDS - 1):
        pl.semaphore_signal(
            barrier, inc=1, device_id={"band": lax.rem(band + shift, BANDS)}, device_id_type=MESH
        )

    def visitors(turn):
        return occ if turn == 0 else visit.at[turn - 1]

    def forward(turn):
        orbital = res[0].reshape(2 * N, N)
        group = visitors(turn)
        pair = jnp.concatenate([group[v].reshape(2 * N, N) * orbital for v in range(2)], axis=1)
        along_z = data_by_table(pair, z_high, z_low)
        modes = table_by_data(y_high, y_low, along_z)
        for v in range(2):
            sbuf[turn, :, v] = modes[:, v * N : (v + 1) * N].reshape(N // 4, 8, N)

    def each_peer(start_copy):
        start_copy(lax.rem(me + GRID // 2, GRID))

        def step(index, carry):
            offset = GRID // 2 - index
            start_copy(lax.rem(me + offset, GRID))
            start_copy(lax.rem(me + (GRID - offset), GRID))
            return carry

        lax.fori_loop(1, GRID // 2, step, 0)

    def send(turn):
        def start_copy(peer):
            pltpu.make_async_remote_copy(
                src_ref=sbuf.at[turn, lax.div(peer, 2), lax.rem(peer, 2)],
                dst_ref=rbuf.at[turn, mine],
                send_sem=send_sem.at[turn],
                recv_sem=recv_sem.at[turn],
                device_id={"grid": peer},
                device_id_type=MESH,
            ).start()

        each_peer(start_copy)
        rbuf[turn, mine] = sbuf[turn, lax.div(me, 2), lax.rem(me, 2)]

    def send_back(turn):
        def start_copy(peer):
            pltpu.make_async_remote_copy(
                src_ref=sback.at[turn, pl.ds(pl.multiple_of(peer * 8, 8), 8)],
                dst_ref=rback.at[turn, lax.div(me, 2), lax.rem(me, 2)],
                send_sem=bsend_sem.at[turn],
                recv_sem=brecv_sem.at[turn],
                device_id={"grid": peer},
                device_id_type=MESH,
            ).start()

        each_peer(start_copy)
        rback[turn, lax.div(me, 2), lax.rem(me, 2)] = sback[turn, mine]

    def wait_all(sem):
        part = rbuf.at[0, pl.ds(0, (GRID - 1) * 8)]
        pltpu.make_async_copy(part, part, sem).wait()

    def columns(turn):
        wait_all(recv_sem.at[turn])
        value = jnp.concatenate(
            [rbuf[turn, pl.ds(row, N, stride=4), :] for row in range(4)], axis=1
        )
        modes = table_by_data(x_high, x_low, value) * coef[...]
        back = table_by_data(x_high, x_low, modes)
        for row in range(4):
            sback[turn, pl.ds(row, N, stride=4), :] = back[:, row * N : (row + 1) * N]

    def inverse(turn):
        wait_all(brecv_sem.at[turn])
        value = jnp.concatenate([rback[turn, :, v].reshape(2 * N, N) for v in range(2)], axis=1)
        along_y = table_by_data(yt_high, yt_low, value)
        potential = data_by_table(along_y, z_high, z_low)
        group = visitors(turn)
        term = group[0].reshape(2 * N, N) * potential[:, :N]
        return term + group[1].reshape(2 * N, N) * potential[:, N:]

    first = lax.div(me, 2) * 4
    square_x = signed_square(lax.broadcasted_iota(jnp.int32, (N, N), 0))
    square_z = signed_square(lax.broadcasted_iota(jnp.int32, (N, N), 1))
    for row in range(4):
        square_y = signed_square(jnp.full((N, N), first + row, jnp.int32))
        q_square = (square_x + square_y + square_z) / (4.0 * screening**2)
        positive = q_square > 0
        safe = jnp.where(positive, q_square, 1.0)
        ratio = jnp.where(positive, (1.0 - jnp.exp(-safe)) / safe, 1.0)
        coef[:, row * N : (row + 1) * N] = (math.pi / screening**2 / CELLS) * ratio
    forward(0)

    pl.semaphore_wait(barrier, GRID - 1 + 4)

    visits = []
    for shift in (1, 2):
        copy = pltpu.make_async_remote_copy(
            src_ref=occ,
            dst_ref=visit.at[shift - 1],
            send_sem=visit_send.at[shift - 1],
            recv_sem=visit_recv.at[shift - 1],
            device_id={"band": lax.rem(band + shift, BANDS)},
            device_id_type=MESH,
        )
        copy.start()
        visits.append(copy)
    send(0)
    visits[0].wait_recv()
    forward(1)
    send(1)
    columns(0)
    send_back(0)
    visits[1].wait_recv()
    forward(2)
    send(2)
    columns(1)
    send_back(1)
    columns(2)
    send_back(2)
    total = inverse(0)
    total = total + inverse(1)
    total = total + inverse(2)
    out[0] = total.reshape(2, N, N)

    for copy in visits:
        copy.wait_send()
    for turn in range(TURNS):
        wait_all(send_sem.at[turn])
        wait_all(bsend_sem.at[turn])


def local(resident, occupied):
    vmem = pl.BlockSpec(memory_space=pltpu.VMEM)
    total = pl.pallas_call(
        kernel,
        out_shape=jax.ShapeDtypeStruct((1, 2, N, N), F32),
        in_specs=[vmem] * 10,
        out_specs=vmem,
        scratch_shapes=[
            pltpu.VMEM((TURNS - 1, 2, 2, N, N), F32),
            pltpu.VMEM((TURNS, GRID // 2, 2, 8, N), F32),
            pltpu.VMEM((TURNS, GRID * 8, N), F32),
            pltpu.VMEM((TURNS, GRID * 8, N), F32),
            pltpu.VMEM((TURNS, GRID // 2, 2, 8, N), F32),
            pltpu.VMEM((N, 4 * N), F32),
            pltpu.SemaphoreType.DMA((TURNS - 1,)),
            pltpu.SemaphoreType.DMA((TURNS - 1,)),
            pltpu.SemaphoreType.DMA((TURNS,)),
            pltpu.SemaphoreType.DMA((TURNS,)),
            pltpu.SemaphoreType.DMA((TURNS,)),
            pltpu.SemaphoreType.DMA((TURNS,)),
        ],
        compiler_params=pltpu.CompilerParams(collective_id=0, has_side_effects=True),
    )(resident, occupied, *[jnp.asarray(table) for table in tables()])
    return -mix_fraction * total


def solution(mesh):
    spec = P("band", "grid", None, None)
    return jax.shard_map(local, mesh=mesh, in_specs=(spec, spec), out_specs=spec, check_vma=False)
```

```python
import functools
import math

import jax
import jax.numpy as jnp
import numpy as np
from jax import lax
from jax.experimental import pallas as pl
from jax.experimental.pallas import tpu as pltpu
from jax.sharding import PartitionSpec as P

N = 128
CELLS = N * N * N
TURNS = 3
BANDS = 16
GRID = 64
LINE = 8
PIECE = N // LINE
screening = 0.05
mix_fraction = 0.25
MESH = pl.DeviceIdType.MESH
F32 = jnp.float32
BF16 = jnp.bfloat16


def split_table(table):
    high = table.astype(np.float32).astype(jnp.bfloat16)
    low = (table - high.astype(np.float64)).astype(np.float32).astype(jnp.bfloat16)
    return [high, low]


def tables():
    index = np.arange(N)
    angle = (index[:, None] * index[None, :] % N) * (2.0 * math.pi / N)
    cas = np.cos(angle) + np.sin(angle)
    along_z = np.kron(np.eye(2), cas)
    along_y = np.zeros((N // 4, 2, 4, 2, N))
    for plane in range(2):
        along_y[:, plane, :, plane, :] = cas.reshape(N // 4, 4, N)
    along_y = along_y.reshape(2 * N, 2 * N)
    out = []
    for table in (along_z, along_y, along_y.T, cas):
        out += split_table(table)
    return out


def halves(value):
    high = value.astype(BF16)
    low = (value - high.astype(F32)).astype(BF16)
    return high, low


def dot(a, b):
    return jnp.dot(a, b, preferred_element_type=F32)


def data_by_table(value, high, low):
    a, b = halves(value)
    return dot(a, high[...]) + (dot(b, high[...]) + dot(a, low[...]))


def table_by_data(high, low, value):
    a, b = halves(value)
    return dot(high[...], a) + (dot(high[...], b) + dot(low[...], a))


def signed_square(index):
    signed = jnp.minimum(index, N - index).astype(F32) * (2.0 * math.pi / N)
    return signed * signed


def kernel(
    res, occ, z_high, z_low, y_high, y_low, yt_high, yt_low, x_high, x_low, out,
    visit, cross, sbuf, rbuf, sback, rback, coef,
    visit_send, visit_recv, cross_send, cross_recv, pass_send, send_sem, recv_sem, bsend_sem, brecv_sem,
):
    band = lax.axis_index("band")
    me = lax.axis_index("grid")
    mine = pl.ds(pl.multiple_of(me * 8, 8), 8)

    barrier = pltpu.get_barrier_semaphore()

    def greet(step, carry):
        pl.semaphore_signal(
            barrier, inc=1, device_id={"grid": lax.rem(me + step, GRID)}, device_id_type=MESH
        )
        return carry

    lax.fori_loop(1, GRID, greet, 0)

    def greet_band(step, carry):
        pl.semaphore_signal(
            barrier, inc=1, device_id={"band": lax.rem(band + step, BANDS)}, device_id_type=MESH
        )
        return carry

    lax.fori_loop(1, BANDS, greet_band, 0)

    def visitors(turn):
        return occ if turn == 0 else visit.at[turn - 1]

    def forward(turn):
        orbital = res[0].reshape(2 * N, N)
        group = visitors(turn)
        pair = jnp.concatenate([group[v].reshape(2 * N, N) * orbital for v in range(2)], axis=1)
        along_z = data_by_table(pair, z_high, z_low)
        modes = table_by_data(y_high, y_low, along_z)
        for v in range(2):
            sbuf[turn, :, v] = modes[:, v * N : (v + 1) * N].reshape(N // 4, 8, N)

    def each_peer(start_copy):
        start_copy(lax.rem(me + GRID // 2, GRID))

        def step(index, carry):
            offset = GRID // 2 - index
            start_copy(lax.rem(me + offset, GRID))
            start_copy(lax.rem(me + (GRID - offset), GRID))
            return carry

        lax.fori_loop(1, GRID // 2, step, 0)

    def send(turn):
        def start_copy(peer):
            pltpu.make_async_remote_copy(
                src_ref=sbuf.at[turn, lax.div(peer, 2), lax.rem(peer, 2)],
                dst_ref=rbuf.at[turn, mine],
                send_sem=send_sem.at[turn],
                recv_sem=recv_sem.at[turn],
                device_id={"grid": peer},
                device_id_type=MESH,
            ).start()

        each_peer(start_copy)
        rbuf[turn, mine] = sbuf[turn, lax.div(me, 2), lax.rem(me, 2)]

    def send_back(turn):
        def start_copy(peer):
            pltpu.make_async_remote_copy(
                src_ref=sback.at[turn, pl.ds(pl.multiple_of(peer * 8, 8), 8)],
                dst_ref=rback.at[turn, lax.div(me, 2), lax.rem(me, 2)],
                send_sem=bsend_sem.at[turn],
                recv_sem=brecv_sem.at[turn],
                device_id={"grid": peer},
                device_id_type=MESH,
            ).start()

        each_peer(start_copy)
        rback[turn, lax.div(me, 2), lax.rem(me, 2)] = sback[turn, mine]

    def wait_all(sem):
        part = rbuf.at[0, pl.ds(0, (GRID - 1) * 8)]
        pltpu.make_async_copy(part, part, sem).wait()

    def columns(turn):
        wait_all(recv_sem.at[turn])
        value = jnp.concatenate(
            [rbuf[turn, pl.ds(row, N, stride=4), :] for row in range(4)], axis=1
        )
        modes = table_by_data(x_high, x_low, value) * coef[...]
        back = table_by_data(x_high, x_low, modes)
        for row in range(4):
            sback[turn, pl.ds(row, N, stride=4), :] = back[:, row * N : (row + 1) * N]

    def inverse(turn):
        wait_all(brecv_sem.at[turn])
        value = jnp.concatenate([rback[turn, :, v].reshape(2 * N, N) for v in range(2)], axis=1)
        along_y = table_by_data(yt_high, yt_low, value)
        potential = data_by_table(along_y, z_high, z_low)
        group = visitors(turn)
        term = group[0].reshape(2 * N, N) * potential[:, :N]
        return term + group[1].reshape(2 * N, N) * potential[:, N:]

    first = lax.div(me, 2) * 4
    square_x = signed_square(lax.broadcasted_iota(jnp.int32, (N, N), 0))
    square_z = signed_square(lax.broadcasted_iota(jnp.int32, (N, N), 1))
    for row in range(4):
        square_y = signed_square(jnp.full((N, N), first + row, jnp.int32))
        q_square = (square_x + square_y + square_z) / (4.0 * screening**2)
        positive = q_square > 0
        safe = jnp.where(positive, q_square, 1.0)
        ratio = jnp.where(positive, (1.0 - jnp.exp(-safe)) / safe, 1.0)
        coef[:, row * N : (row + 1) * N] = (math.pi / screening**2 / CELLS) * ratio
    forward(0)

    pl.semaphore_wait(barrier, GRID - 1 + BANDS - 1)

    place = lax.rem(band, LINE)
    side = lax.div(band, LINE)
    whole = visit.at[0]

    def shift_copy(shift):
        return pltpu.make_async_remote_copy(
            src_ref=occ,
            dst_ref=visit.at[shift - 1],
            send_sem=visit_send.at[shift - 1],
            recv_sem=visit_recv.at[shift - 1],
            device_id={"band": band + shift},
            device_id_type=MESH,
        )

    def piece(index):
        return pl.ds(pl.multiple_of(index * PIECE, PIECE), PIECE)

    for late in range(2):
        @pl.when(place == LINE - 1 - late)
        def _():
            def step(index, carry):
                pltpu.make_async_remote_copy(
                    src_ref=occ.at[:, :, piece(index)],
                    dst_ref=cross.at[late],
                    send_sem=cross_send.at[late],
                    recv_sem=cross_recv.at[late],
                    device_id={"band": (1 - side) * LINE + index},
                    device_id_type=MESH,
                ).start()
                return carry

            lax.fori_loop(0, LINE, step, 0)

    for shift in (1, 2):
        @pl.when(place + shift < LINE)
        def _():
            shift_copy(shift).start()

    def pass_on(late, target, slot, order):
        part = visit.at[slot, :, :, piece(place)]

        @pl.when(place == target)
        def _():
            pltpu.make_async_copy(cross.at[late], part, visit_recv.at[slot]).start()

        @pl.when(place != target)
        def _():
            pltpu.make_async_remote_copy(
                src_ref=cross.at[late],
                dst_ref=part,
                send_sem=pass_send.at[order],
                recv_sem=visit_recv.at[slot],
                device_id={"band": side * LINE + target},
                device_id_type=MESH,
            ).start()

    passes = ((0, 0, 0), (0, 1, 1), (1, 0, 1))

    def relay():
        pltpu.make_async_copy(cross.at[0], cross.at[0], cross_recv.at[0]).wait()
        pass_on(*passes[0], 0)
        pass_on(*passes[1], 1)
        pltpu.make_async_copy(cross.at[1], cross.at[1], cross_recv.at[1]).wait()
        pass_on(*passes[2], 2)

    def next_turn(turn):
        pltpu.make_async_copy(whole, whole, visit_recv.at[turn - 1]).wait()
        forward(turn)
        send(turn)

    send(0)
    relay()

    @pl.when(place > 0)
    def _():
        next_turn(1)

    columns(0)
    send_back(0)

    @pl.when(place == 0)
    def _():
        next_turn(1)

    next_turn(2)
    columns(1)
    send_back(1)
    columns(2)
    send_back(2)
    total = inverse(0)
    total = total + inverse(1)
    total = total + inverse(2)
    out[0] = total.reshape(2, N, N)

    for shift in (1, 2):
        @pl.when(place + shift < LINE)
        def _():
            shift_copy(shift).wait_send()

    for late in range(2):
        @pl.when(place == LINE - 1 - late)
        def _():
            pltpu.make_async_copy(whole, whole, cross_send.at[late]).wait()

    for order, (late, target, slot) in enumerate(passes):
        @pl.when(place != target)
        def _():
            pltpu.make_async_copy(cross.at[late], cross.at[late], pass_send.at[order]).wait()

    for turn in range(TURNS):
        wait_all(send_sem.at[turn])
        wait_all(bsend_sem.at[turn])


def local(resident, occupied):
    vmem = pl.BlockSpec(memory_space=pltpu.VMEM)
    total = pl.pallas_call(
        kernel,
        out_shape=jax.ShapeDtypeStruct((1, 2, N, N), F32),
        in_specs=[vmem] * 10,
        out_specs=vmem,
        scratch_shapes=[
            pltpu.VMEM((TURNS - 1, 2, 2, N, N), F32),
            pltpu.VMEM((2, 2, 2, PIECE, N), F32),
            pltpu.VMEM((TURNS, GRID // 2, 2, 8, N), F32),
            pltpu.VMEM((TURNS, GRID * 8, N), F32),
            pltpu.VMEM((TURNS, GRID * 8, N), F32),
            pltpu.VMEM((TURNS, GRID // 2, 2, 8, N), F32),
            pltpu.VMEM((N, 4 * N), F32),
            pltpu.SemaphoreType.DMA((TURNS - 1,)),
            pltpu.SemaphoreType.DMA((TURNS - 1,)),
            pltpu.SemaphoreType.DMA((2,)),
            pltpu.SemaphoreType.DMA((2,)),
            pltpu.SemaphoreType.DMA((3,)),
            pltpu.SemaphoreType.DMA((TURNS,)),
            pltpu.SemaphoreType.DMA((TURNS,)),
            pltpu.SemaphoreType.DMA((TURNS,)),
            pltpu.SemaphoreType.DMA((TURNS,)),
        ],
        compiler_params=pltpu.CompilerParams(collective_id=0, has_side_effects=True),
    )(resident, occupied, *[jnp.asarray(table) for table in tables()])
    return -mix_fraction * total


def solution(mesh):
    spec = P("band", "grid", None, None)
    return jax.shard_map(local, mesh=mesh, in_specs=(spec, spec), out_specs=spec, check_vma=False)
```

```python
import functools
import math

import jax
import jax.numpy as jnp
import numpy as np
from jax import lax
from jax.experimental import pallas as pl
from jax.experimental.pallas import tpu as pltpu
from jax.sharding import PartitionSpec as P

N = 128
CELLS = N * N * N
TURNS = 3
BANDS = 16
GRID = 64
LINE = 8
PIECE = N // LINE
screening = 0.05
mix_fraction = 0.25
MESH = pl.DeviceIdType.MESH
F32 = jnp.float32
BF16 = jnp.bfloat16


def split_table(table):
    high = table.astype(np.float32).astype(jnp.bfloat16)
    low = (table - high.astype(np.float64)).astype(np.float32).astype(jnp.bfloat16)
    return [high, low]


def tables():
    index = np.arange(N)
    angle = (index[:, None] * index[None, :] % N) * (2.0 * math.pi / N)
    cas = np.cos(angle) + np.sin(angle)
    along_z = np.kron(np.eye(2), cas)
    along_y = np.zeros((N // 4, 2, 4, 2, N))
    for plane in range(2):
        along_y[:, plane, :, plane, :] = cas.reshape(N // 4, 4, N)
    along_y = along_y.reshape(2 * N, 2 * N)
    out = []
    for table in (along_z, along_y, along_y.T, cas):
        out += split_table(table)
    return out


def halves(value):
    high = value.astype(BF16)
    low = (value - high.astype(F32)).astype(BF16)
    return high, low


def dot(a, b):
    return jnp.dot(a, b, preferred_element_type=F32)


def data_by_table(value, high, low):
    a, b = halves(value)
    return dot(a, high[...]) + (dot(b, high[...]) + dot(a, low[...]))


def table_by_data(high, low, value):
    a, b = halves(value)
    return dot(high[...], a) + (dot(high[...], b) + dot(low[...], a))


def signed_square(index):
    signed = jnp.minimum(index, N - index).astype(F32) * (2.0 * math.pi / N)
    return signed * signed


def kernel(
    res, occ, z_high, z_low, y_high, y_low, yt_high, yt_low, x_high, x_low, out,
    visit, cross, sbuf, rbuf, sback, rback, coef,
    visit_send, visit_recv, cross_send, cross_recv, pass_send, send_sem, recv_sem, bsend_sem, brecv_sem,
):
    band = lax.axis_index("band")
    me = lax.axis_index("grid")
    mine = pl.ds(pl.multiple_of(me * 8, 8), 8)

    barrier = pltpu.get_barrier_semaphore()

    def greet(step, carry):
        pl.semaphore_signal(
            barrier, inc=1, device_id={"grid": lax.rem(me + step, GRID)}, device_id_type=MESH
        )
        return carry

    lax.fori_loop(1, GRID, greet, 0)

    def greet_band(step, carry):
        pl.semaphore_signal(
            barrier, inc=1, device_id={"band": lax.rem(band + step, BANDS)}, device_id_type=MESH
        )
        return carry

    lax.fori_loop(1, BANDS, greet_band, 0)

    def visitors(turn):
        return occ if turn == 0 else visit.at[turn - 1]

    def forward(turn):
        orbital = res[0].reshape(2 * N, N)
        group = visitors(turn)
        pair = jnp.concatenate([group[v].reshape(2 * N, N) * orbital for v in range(2)], axis=1)
        along_z = data_by_table(pair, z_high, z_low)
        modes = table_by_data(y_high, y_low, along_z)
        for v in range(2):
            sbuf[turn, :, v] = modes[:, v * N : (v + 1) * N].reshape(N // 4, 8, N)

    def each_peer(start_copy):
        start_copy(lax.rem(me + GRID // 2, GRID))

        def step(index, carry):
            offset = GRID // 2 - index
            start_copy(lax.rem(me + offset, GRID))
            start_copy(lax.rem(me + (GRID - offset), GRID))
            return carry

        lax.fori_loop(1, GRID // 2, step, 0)

    def send(turn):
        def start_copy(peer):
            pltpu.make_async_remote_copy(
                src_ref=sbuf.at[turn, lax.div(peer, 2), lax.rem(peer, 2)],
                dst_ref=rbuf.at[turn, mine],
                send_sem=send_sem.at[turn],
                recv_sem=recv_sem.at[turn],
                device_id={"grid": peer},
                device_id_type=MESH,
            ).start()

        each_peer(start_copy)
        rbuf[turn, mine] = sbuf[turn, lax.div(me, 2), lax.rem(me, 2)]

    def send_back(turn):
        def start_copy(peer):
            pltpu.make_async_remote_copy(
                src_ref=sback.at[turn, pl.ds(pl.multiple_of(peer * 8, 8), 8)],
                dst_ref=rback.at[turn, lax.div(me, 2), lax.rem(me, 2)],
                send_sem=bsend_sem.at[turn],
                recv_sem=brecv_sem.at[turn],
                device_id={"grid": peer},
                device_id_type=MESH,
            ).start()

        each_peer(start_copy)
        rback[turn, lax.div(me, 2), lax.rem(me, 2)] = sback[turn, mine]

    def wait_all(sem):
        part = rbuf.at[0, pl.ds(0, (GRID - 1) * 8)]
        pltpu.make_async_copy(part, part, sem).wait()

    def factors():
        first = lax.div(me, 2) * 4
        square_x = signed_square(lax.broadcasted_iota(jnp.int32, (N, N), 0))
        square_z = signed_square(lax.broadcasted_iota(jnp.int32, (N, N), 1))
        for row in range(4):
            square_y = signed_square(jnp.full((N, N), first + row, jnp.int32))
            q_square = (square_x + square_y + square_z) / (4.0 * screening**2)
            positive = q_square > 0
            safe = jnp.where(positive, q_square, 1.0)
            ratio = jnp.where(positive, (1.0 - jnp.exp(-safe)) / safe, 1.0)
            coef[:, row * N : (row + 1) * N] = (math.pi / screening**2 / CELLS) * ratio

    def columns(turn):
        wait_all(recv_sem.at[turn])
        value = jnp.concatenate(
            [rbuf[turn, pl.ds(row, N, stride=4), :] for row in range(4)], axis=1
        )
        modes = table_by_data(x_high, x_low, value) * coef[...]
        back = table_by_data(x_high, x_low, modes)
        for row in range(4):
            sback[turn, pl.ds(row, N, stride=4), :] = back[:, row * N : (row + 1) * N]

    def inverse(turn):
        wait_all(brecv_sem.at[turn])
        value = jnp.concatenate([rback[turn, :, v].reshape(2 * N, N) for v in range(2)], axis=1)
        along_y = table_by_data(yt_high, yt_low, value)
        potential = data_by_table(along_y, z_high, z_low)
        group = visitors(turn)
        term = group[0].reshape(2 * N, N) * potential[:, :N]
        return term + group[1].reshape(2 * N, N) * potential[:, N:]

    forward(0)

    pl.semaphore_wait(barrier, GRID - 1 + BANDS - 1)

    place = lax.rem(band, LINE)
    side = lax.div(band, LINE)
    whole = visit.at[0]

    def hand_on(source, slot):
        return pltpu.make_async_remote_copy(
            src_ref=source,
            dst_ref=visit.at[slot],
            send_sem=visit_send.at[slot],
            recv_sem=visit_recv.at[slot],
            device_id={"band": band + 1},
            device_id_type=MESH,
        )

    first_hand = hand_on(occ, 0)
    second_hand = hand_on(visit.at[0], 1)
    inner = jnp.logical_and(place > 0, place < LINE - 1)

    def piece(index):
        return pl.ds(pl.multiple_of(index * PIECE, PIECE), PIECE)

    for late in range(2):
        @pl.when(place == LINE - 1 - late)
        def _():
            def step(index, carry):
                pltpu.make_async_remote_copy(
                    src_ref=occ.at[:, :, piece(index)],
                    dst_ref=cross.at[late],
                    send_sem=cross_send.at[late],
                    recv_sem=cross_recv.at[late],
                    device_id={"band": (1 - side) * LINE + index},
                    device_id_type=MESH,
                ).start()
                return carry

            lax.fori_loop(0, LINE, step, 0)

    @pl.when(place < LINE - 1)
    def _():
        first_hand.start()

    def pass_on(late, target, slot, order):
        part = visit.at[slot, :, :, piece(place)]

        @pl.when(place == target)
        def _():
            pltpu.make_async_copy(cross.at[late], part, visit_recv.at[slot]).start()

        @pl.when(place != target)
        def _():
            pltpu.make_async_remote_copy(
                src_ref=cross.at[late],
                dst_ref=part,
                send_sem=pass_send.at[order],
                recv_sem=visit_recv.at[slot],
                device_id={"band": side * LINE + target},
                device_id_type=MESH,
            ).start()

    passes = ((0, 0, 0), (1, 0, 1), (0, 1, 1))

    def relay(late):
        pltpu.make_async_copy(cross.at[late], cross.at[late], cross_recv.at[late]).wait()
        pass_on(*passes[late], late)

    def next_turn(turn):
        pltpu.make_async_copy(whole, whole, visit_recv.at[turn - 1]).wait()
        forward(turn)
        send(turn)

    send(0)
    factors()
    relay(0)

    @pl.when(place > 0)
    def _():
        next_turn(1)

    relay(1)
    pass_on(*passes[2], 2)

    @pl.when(inner)
    def _():
        second_hand.start()

    columns(0)
    send_back(0)

    @pl.when(place == 0)
    def _():
        next_turn(1)

    next_turn(2)
    columns(1)
    send_back(1)
    columns(2)
    send_back(2)
    total = inverse(0)
    total = total + inverse(1)
    total = total + inverse(2)
    out[0] = total.reshape(2, N, N)

    @pl.when(place < LINE - 1)
    def _():
        first_hand.wait_send()

    @pl.when(inner)
    def _():
        second_hand.wait_send()

    for late in range(2):
        @pl.when(place == LINE - 1 - late)
        def _():
            pltpu.make_async_copy(whole, whole, cross_send.at[late]).wait()

    for order, (late, target, slot) in enumerate(passes):
        @pl.when(place != target)
        def _():
            pltpu.make_async_copy(cross.at[late], cross.at[late], pass_send.at[order]).wait()

    for turn in range(TURNS):
        wait_all(send_sem.at[turn])
        wait_all(bsend_sem.at[turn])


def local(resident, occupied):
    vmem = pl.BlockSpec(memory_space=pltpu.VMEM)
    total = pl.pallas_call(
        kernel,
        out_shape=jax.ShapeDtypeStruct((1, 2, N, N), F32),
        in_specs=[vmem] * 10,
        out_specs=vmem,
        scratch_shapes=[
            pltpu.VMEM((TURNS - 1, 2, 2, N, N), F32),
            pltpu.VMEM((2, 2, 2, PIECE, N), F32),
            pltpu.VMEM((TURNS, GRID // 2, 2, 8, N), F32),
            pltpu.VMEM((TURNS, GRID * 8, N), F32),
            pltpu.VMEM((TURNS, GRID * 8, N), F32),
            pltpu.VMEM((TURNS, GRID // 2, 2, 8, N), F32),
            pltpu.VMEM((N, 4 * N), F32),
            pltpu.SemaphoreType.DMA((TURNS - 1,)),
            pltpu.SemaphoreType.DMA((TURNS - 1,)),
            pltpu.SemaphoreType.DMA((2,)),
            pltpu.SemaphoreType.DMA((2,)),
            pltpu.SemaphoreType.DMA((3,)),
            pltpu.SemaphoreType.DMA((TURNS,)),
            pltpu.SemaphoreType.DMA((TURNS,)),
            pltpu.SemaphoreType.DMA((TURNS,)),
            pltpu.SemaphoreType.DMA((TURNS,)),
        ],
        compiler_params=pltpu.CompilerParams(collective_id=0, has_side_effects=True),
    )(resident, occupied, *[jnp.asarray(table) for table in tables()])
    return -mix_fraction * total


def solution(mesh):
    spec = P("band", "grid", None, None)
    return jax.shard_map(local, mesh=mesh, in_specs=(spec, spec), out_specs=spec, check_vma=False)
```

```python
import functools
import math

import jax
import jax.numpy as jnp
import numpy as np
from jax import lax
from jax.experimental import pallas as pl
from jax.experimental.pallas import tpu as pltpu
from jax.sharding import PartitionSpec as P

N = 128
CELLS = N * N * N
TURNS = 3
BANDS = 16
GRID = 64
LINE = 8
VIA = 2
VIAS = 4
PIECE = N // VIAS
screening = 0.05
mix_fraction = 0.25
MESH = pl.DeviceIdType.MESH
F32 = jnp.float32
BF16 = jnp.bfloat16


def split_table(table):
    high = table.astype(np.float32).astype(jnp.bfloat16)
    low = (table - high.astype(np.float64)).astype(np.float32).astype(jnp.bfloat16)
    return [high, low]


def tables():
    index = np.arange(N)
    angle = (index[:, None] * index[None, :] % N) * (2.0 * math.pi / N)
    cas = np.cos(angle) + np.sin(angle)
    along_z = np.kron(np.eye(2), cas)
    along_y = np.zeros((N // 4, 2, 4, 2, N))
    for plane in range(2):
        along_y[:, plane, :, plane, :] = cas.reshape(N // 4, 4, N)
    along_y = along_y.reshape(2 * N, 2 * N)
    out = []
    for table in (along_z, along_y, along_y.T, cas):
        out += split_table(table)
    return out


def halves(value):
    high = value.astype(BF16)
    low = (value - high.astype(F32)).astype(BF16)
    return high, low


def dot(a, b):
    return jnp.dot(a, b, preferred_element_type=F32)


def data_by_table(value, high, low):
    a, b = halves(value)
    return dot(a, high[...]) + (dot(b, high[...]) + dot(a, low[...]))


def table_by_data(high, low, value):
    a, b = halves(value)
    return dot(high[...], a) + (dot(high[...], b) + dot(low[...], a))


def signed_square(index):
    signed = jnp.minimum(index, N - index).astype(F32) * (2.0 * math.pi / N)
    return signed * signed


def kernel(
    res, occ, z_high, z_low, y_high, y_low, yt_high, yt_low, x_high, x_low, out,
    visit, cross, sbuf, rbuf, sback, rback, coef,
    visit_send, visit_recv, cross_send, cross_recv, pass_send, send_sem, recv_sem, bsend_sem, brecv_sem,
):
    band = lax.axis_index("band")
    me = lax.axis_index("grid")
    mine = pl.ds(pl.multiple_of(me * 8, 8), 8)

    barrier = pltpu.get_barrier_semaphore()

    def greet(step, carry):
        pl.semaphore_signal(
            barrier, inc=1, device_id={"grid": lax.rem(me + step, GRID)}, device_id_type=MESH
        )
        return carry

    lax.fori_loop(1, GRID, greet, 0)

    def greet_band(step, carry):
        pl.semaphore_signal(
            barrier, inc=1, device_id={"band": lax.rem(band + step, BANDS)}, device_id_type=MESH
        )
        return carry

    lax.fori_loop(1, BANDS, greet_band, 0)

    def visitors(turn):
        return occ if turn == 0 else visit.at[turn - 1]

    def forward(turn):
        orbital = res[0].reshape(2 * N, N)
        group = visitors(turn)
        pair = jnp.concatenate([group[v].reshape(2 * N, N) * orbital for v in range(2)], axis=1)
        along_z = data_by_table(pair, z_high, z_low)
        modes = table_by_data(y_high, y_low, along_z)
        for v in range(2):
            sbuf[turn, :, v] = modes[:, v * N : (v + 1) * N].reshape(N // 4, 8, N)

    def each_peer(start_copy):
        start_copy(lax.rem(me + GRID // 2, GRID))

        def step(index, carry):
            offset = GRID // 2 - index
            start_copy(lax.rem(me + offset, GRID))
            start_copy(lax.rem(me + (GRID - offset), GRID))
            return carry

        lax.fori_loop(1, GRID // 2, step, 0)

    def send(turn):
        def start_copy(peer):
            pltpu.make_async_remote_copy(
                src_ref=sbuf.at[turn, lax.div(peer, 2), lax.rem(peer, 2)],
                dst_ref=rbuf.at[turn, mine],
                send_sem=send_sem.at[turn],
                recv_sem=recv_sem.at[turn],
                device_id={"grid": peer},
                device_id_type=MESH,
            ).start()

        each_peer(start_copy)
        rbuf[turn, mine] = sbuf[turn, lax.div(me, 2), lax.rem(me, 2)]

    def send_back(turn):
        def start_copy(peer):
            pltpu.make_async_remote_copy(
                src_ref=sback.at[turn, pl.ds(pl.multiple_of(peer * 8, 8), 8)],
                dst_ref=rback.at[turn, lax.div(me, 2), lax.rem(me, 2)],
                send_sem=bsend_sem.at[turn],
                recv_sem=brecv_sem.at[turn],
                device_id={"grid": peer},
                device_id_type=MESH,
            ).start()

        each_peer(start_copy)
        rback[turn, lax.div(me, 2), lax.rem(me, 2)] = sback[turn, mine]

    def wait_all(sem):
        part = rbuf.at[0, pl.ds(0, (GRID - 1) * 8)]
        pltpu.make_async_copy(part, part, sem).wait()

    def factors():
        first = lax.div(me, 2) * 4
        square_x = signed_square(lax.broadcasted_iota(jnp.int32, (N, N), 0))
        square_z = signed_square(lax.broadcasted_iota(jnp.int32, (N, N), 1))
        for row in range(4):
            square_y = signed_square(jnp.full((N, N), first + row, jnp.int32))
            q_square = (square_x + square_y + square_z) / (4.0 * screening**2)
            positive = q_square > 0
            safe = jnp.where(positive, q_square, 1.0)
            ratio = jnp.where(positive, (1.0 - jnp.exp(-safe)) / safe, 1.0)
            coef[:, row * N : (row + 1) * N] = (math.pi / screening**2 / CELLS) * ratio

    def columns(turn):
        wait_all(recv_sem.at[turn])
        value = jnp.concatenate(
            [rbuf[turn, pl.ds(row, N, stride=4), :] for row in range(4)], axis=1
        )
        modes = table_by_data(x_high, x_low, value) * coef[...]
        back = table_by_data(x_high, x_low, modes)
        for row in range(4):
            sback[turn, pl.ds(row, N, stride=4), :] = back[:, row * N : (row + 1) * N]

    def inverse(turn):
        wait_all(brecv_sem.at[turn])
        value = jnp.concatenate([rback[turn, :, v].reshape(2 * N, N) for v in range(2)], axis=1)
        along_y = table_by_data(yt_high, yt_low, value)
        potential = data_by_table(along_y, z_high, z_low)
        group = visitors(turn)
        term = group[0].reshape(2 * N, N) * potential[:, :N]
        return term + group[1].reshape(2 * N, N) * potential[:, N:]

    forward(0)

    pl.semaphore_wait(barrier, GRID - 1 + BANDS - 1)

    place = lax.rem(band, LINE)
    side = lax.div(band, LINE)
    whole = visit.at[0]

    def hand_on(source, slot):
        return pltpu.make_async_remote_copy(
            src_ref=source,
            dst_ref=visit.at[slot],
            send_sem=visit_send.at[slot],
            recv_sem=visit_recv.at[slot],
            device_id={"band": band + 1},
            device_id_type=MESH,
        )

    first_hand = hand_on(occ, 0)
    second_hand = hand_on(visit.at[0], 1)
    inner = jnp.logical_and(place > 0, place < LINE - 1)

    def piece(index):
        return pl.ds(pl.multiple_of(index * PIECE, PIECE), PIECE)

    for late in range(2):
        @pl.when(place == LINE - 1 - late)
        def _():
            def step(index, carry):
                pltpu.make_async_remote_copy(
                    src_ref=occ.at[:, :, piece(index)],
                    dst_ref=cross.at[late],
                    send_sem=cross_send.at[late],
                    recv_sem=cross_recv.at[late],
                    device_id={"band": (1 - side) * LINE + VIA + index},
                    device_id_type=MESH,
                ).start()
                return carry

            lax.fori_loop(0, VIAS, step, 0)

    @pl.when(place < LINE - 1)
    def _():
        first_hand.start()

    via = jnp.logical_and(place >= VIA, place < VIA + VIAS)

    def pass_on(late, target, slot, order):
        pltpu.make_async_remote_copy(
            src_ref=cross.at[late],
            dst_ref=visit.at[slot, :, :, piece(place - VIA)],
            send_sem=pass_send.at[order],
            recv_sem=visit_recv.at[slot],
            device_id={"band": side * LINE + target},
            device_id_type=MESH,
        ).start()

    passes = ((0, 0, 0), (1, 0, 1), (0, 1, 1))

    def relay(late):
        pltpu.make_async_copy(cross.at[late], cross.at[late], cross_recv.at[late]).wait()
        pass_on(*passes[late], late)

    def next_turn(turn):
        pltpu.make_async_copy(whole, whole, visit_recv.at[turn - 1]).wait()
        forward(turn)
        send(turn)

    send(0)
    factors()

    @pl.when(via)
    def _():
        relay(0)
        relay(1)
        pass_on(*passes[2], 2)

    @pl.when(place > 0)
    def _():
        next_turn(1)

    @pl.when(inner)
    def _():
        second_hand.start()

    columns(0)
    send_back(0)

    @pl.when(place == 0)
    def _():
        next_turn(1)

    next_turn(2)
    columns(1)
    send_back(1)
    columns(2)
    send_back(2)
    total = inverse(0)
    total = total + inverse(1)
    total = total + inverse(2)
    out[0] = total.reshape(2, N, N)

    @pl.when(place < LINE - 1)
    def _():
        first_hand.wait_send()

    @pl.when(inner)
    def _():
        second_hand.wait_send()

    for late in range(2):
        @pl.when(place == LINE - 1 - late)
        def _():
            pltpu.make_async_copy(whole, whole, cross_send.at[late]).wait()

    @pl.when(via)
    def _():
        for order, (late, target, slot) in enumerate(passes):
            pltpu.make_async_copy(cross.at[late], cross.at[late], pass_send.at[order]).wait()

    for turn in range(TURNS):
        wait_all(send_sem.at[turn])
        wait_all(bsend_sem.at[turn])


def local(resident, occupied):
    vmem = pl.BlockSpec(memory_space=pltpu.VMEM)
    total = pl.pallas_call(
        kernel,
        out_shape=jax.ShapeDtypeStruct((1, 2, N, N), F32),
        in_specs=[vmem] * 10,
        out_specs=vmem,
        scratch_shapes=[
            pltpu.VMEM((TURNS - 1, 2, 2, N, N), F32),
            pltpu.VMEM((2, 2, 2, PIECE, N), F32),
            pltpu.VMEM((TURNS, GRID // 2, 2, 8, N), F32),
            pltpu.VMEM((TURNS, GRID * 8, N), F32),
            pltpu.VMEM((TURNS, GRID * 8, N), F32),
            pltpu.VMEM((TURNS, GRID // 2, 2, 8, N), F32),
            pltpu.VMEM((N, 4 * N), F32),
            pltpu.SemaphoreType.DMA((TURNS - 1,)),
            pltpu.SemaphoreType.DMA((TURNS - 1,)),
            pltpu.SemaphoreType.DMA((2,)),
            pltpu.SemaphoreType.DMA((2,)),
            pltpu.SemaphoreType.DMA((3,)),
            pltpu.SemaphoreType.DMA((TURNS,)),
            pltpu.SemaphoreType.DMA((TURNS,)),
            pltpu.SemaphoreType.DMA((TURNS,)),
            pltpu.SemaphoreType.DMA((TURNS,)),
        ],
        compiler_params=pltpu.CompilerParams(collective_id=0, has_side_effects=True),
    )(resident, occupied, *[jnp.asarray(table) for table in tables()])
    return -mix_fraction * total


def solution(mesh):
    spec = P("band", "grid", None, None)
    return jax.shard_map(local, mesh=mesh, in_specs=(spec, spec), out_specs=spec, check_vma=False)
```
